512 devices in a mesh: dp: 32 (over y_lo, z), row: 4 (over x), col: 4 (over y_hi, core).
Axes of the slice: x: 4, y: 8 (y_hi: 2, y_lo: 4; y = y_hi * 4 + y_lo), z: 8, core: 2. Of those that a mesh axis runs over, the one named last changes fastest.
Arguments:
- query_out: bfloat16 [6144, 4096], P(('dp', 'row'), 'col'), may hold values from -6 to 6
- query_in: bfloat16 [6144, 4096], P(('dp', 'col')), may hold values from -6 to 6
- out_basis: bfloat16 [4096, 4096], P('col', ('dp', 'row')), may hold values from -0.09375 to 0.09375
- in_basis: bfloat16 [4096, 4096], P(('dp', 'row'), 'col'), may hold values from -0.09375 to 0.09375
- eigvals: float32 [4096, 4096], P(('dp', 'row'), 'col'), may hold values from 16 to 1024
- train_out: bfloat16 [6144, 4096], P(('dp', 'row'), 'col'), may hold values from -0.09375 to 0.09375
- train_in: bfloat16 [6144, 4096], P(('dp', 'col')), may hold values from -0.09375 to 0.09375
Outputs:
- precond: float32 [4096, 4096], P(('dp', 'row'), 'col')
- scores: float32 [6144], P('dp')
The draws below stay inside these ranges and needn't reach their ends.
All inputs are finite; a program needn't handle non-finite values.
Results may differ from the reference program's by a relative error of at most 0.028.
Values may be sent and summed in bfloat16 or wider, within the bound.
No kernel may reach another device: no remote copies, remote signals or barrier semaphores. Data moves between devices by JAX's collectives and lax.ppermute only.
A program may use at most 64 MiB of HBM per device.

```python
import math
import jax
import jax.numpy as jnp
from jax import lax

DO = 4096
DI = 4096
TOK_DEV = 192
TOKENS = 6144
N_DP = 32
N_ROW = 4
N_COL = 4


def levels(rng, extent, cuts, smallest, high):
    def one(axis_at, shards_of):
        heights = jax.random.uniform(jax.random.fold_in(jax.random.fold_in(rng, 6), axis_at), (shards_of,), jnp.float32, smallest / len(cuts), high / len(cuts))
        return jnp.repeat(jnp.exp(heights), extent[axis_at] // shards_of).reshape((-1,) + (1,) * (len(extent) - axis_at - 1))

    factor_of = one(*cuts[0])
    for cut in cuts[1:]:
        factor_of = factor_of * one(*cut)
    return factor_of


def gaussian(own_key, dims, deviation, limit, split=(), held_as=jnp.bfloat16):
    result = deviation * jax.random.normal(own_key, dims, jnp.float32)
    if split:
        result = result * levels(own_key, dims, split, -0.22, 0.18)
    return jnp.clip(result, -limit, limit).astype(held_as)


def setup_inputs(seed: int = 0) -> dict:
    streams_of = jax.random.split(jax.random.key(seed), 8)
    query_out = gaussian(streams_of[0], (TOKENS, DO), 1.0, 6.0, ((0, 128), (1, 4)))
    query_in = gaussian(streams_of[1], (TOKENS, DI), 1.0, 6.0, ((0, 128),))
    out_basis = gaussian(streams_of[2], (DO, DO), DO ** -0.5, 0.09375, ((0, 4), (1, 128)))
    in_basis = gaussian(streams_of[3], (DI, DI), DI ** -0.5, 0.09375, ((0, 128), (1, 4)))
    eigvals = jnp.clip(jnp.exp(math.log(1024.0) - 4.158883 * jax.random.uniform(streams_of[4], (DO, DI), jnp.float32) ** levels(streams_of[4], (DO, DI), ((0, 128), (1, 4)), -0.2, 0.2)), 16.0, 1024.0)
    train_out = gaussian(streams_of[5], (TOKENS, DO), 0.015625, 0.09375, ((0, 128), (1, 4)))
    train_in = gaussian(streams_of[6], (TOKENS, DI), 0.015625, 0.09375, ((0, 128),))
    return dict(query_out=query_out, query_in=query_in, out_basis=out_basis, in_basis=in_basis, eigvals=eigvals, train_out=train_out, train_in=train_in)


damping = 1.0


def rounded(value):
    return lax.optimization_barrier(value.astype(jnp.bfloat16)).astype(jnp.float32)


def rotate_out(tok_rows, basis):
    width = DO // N_COL
    summed = jnp.zeros((tok_rows.shape[0], DO), jnp.float32)
    for block in range(N_COL):
        partial_sum = jnp.dot(tok_rows[:, block * width:(block + 1) * width], basis[block * width:(block + 1) * width], preferred_element_type=jnp.float32)
        summed = summed + rounded(partial_sum)
    return summed.astype(jnp.bfloat16)


def rotate_in(tok_rows, basis):
    sub_width = DI // (N_DP * N_ROW)
    count_rows = tok_rows.shape[0]
    split_rows = tok_rows.reshape(count_rows, N_DP, N_ROW, sub_width)
    split_basis = basis.reshape(N_DP, N_ROW, sub_width, DI)
    summed = jnp.zeros((count_rows, DI), jnp.float32)
    for block in range(N_ROW):
        picked = split_rows[:, :, block, :].reshape(count_rows, N_DP * sub_width)
        panel_rows = split_basis[:, block].reshape(N_DP * sub_width, DI)
        partial_sum = jnp.dot(picked, panel_rows, preferred_element_type=jnp.float32)
        summed = summed + rounded(partial_sum)
    return summed.astype(jnp.bfloat16)


def reference(query_out, query_in, out_basis, in_basis, eigvals, train_out, train_in):
    query_rot = rotate_out(query_out, out_basis).reshape(N_DP, TOK_DEV, DO)
    query_inr = rotate_in(query_in, in_basis).reshape(N_DP, TOK_DEV, DI)

    def add_group(summed, pair):
        left_part, right_part = pair
        partial_sum = lax.dot_general(left_part, right_part, (((0,), (0,)), ((), ())), preferred_element_type=jnp.float32)
        return summed + rounded(partial_sum), None

    grad, _ = lax.scan(add_group, jnp.zeros((DO, DI), jnp.float32), (query_rot, query_inr))
    precond = grad / (eigvals + damping)
    shared = precond.astype(jnp.bfloat16)
    train_rot = rotate_out(train_out, out_basis)
    train_inr = rotate_in(train_in, in_basis)
    mixed = jnp.dot(train_rot, shared, preferred_element_type=jnp.float32)
    scores = jnp.sum(mixed * train_inr.astype(jnp.float32), axis=1)
    return precond, scores
```

```python
import jax
import jax.numpy as jnp
from jax import lax
from jax.sharding import Mesh, PartitionSpec as P

damping = 1.0
f32, bf16 = jnp.float32, jnp.bfloat16
DP = ("y", "z")
COL = ("h", "c")


def exchange(blocks, axes):
    return lax.all_to_all(blocks, axes, 0, 0, tiled=True)


def gather(block, axes):
    count = lax.axis_size(axes)
    return exchange(jnp.broadcast_to(block[None], (count,) + block.shape), axes)


def total(blocks):
    return jnp.sum(blocks.astype(f32), axis=0)


def all_sum(partial, axes):
    count = lax.axis_size(axes)
    two, tokens, width = partial.shape
    parts = partial.astype(bf16).reshape(two, count, tokens // count, width)
    mine = total(exchange(parts.transpose(1, 0, 2, 3), axes)).astype(bf16)
    return gather(mine, axes).transpose(1, 0, 2, 3).reshape(two, tokens, width)


def gather_tokens(block, axes):
    two, rows, width = block.shape
    return gather(block, axes).transpose(1, 0, 2, 3).reshape(two, -1, width)


def dot(left, right, dims):
    return lax.dot_general(left, right, (dims, ((), ())), preferred_element_type=f32)


def per_device(query_out, query_in, out_basis, in_basis, eigvals, train_out, train_in):
    groups = lax.axis_size(DP)
    row_count = lax.axis_size("x")
    rows_own = eigvals.shape[0]

    both = gather(jnp.concatenate([out_basis.T, in_basis], axis=0), DP)
    panel_out = both[:, :rows_own].reshape(groups * rows_own, -1)
    panel_in = both[:, rows_own:].reshape(groups * rows_own, -1)

    tok_out = gather_tokens(jnp.stack([query_out, train_out]), "x")
    split = jnp.stack([query_in, train_in])
    rows = split.shape[1]
    split = split.reshape(2, rows, groups, row_count, -1)
    picked = lax.dynamic_index_in_dim(split, lax.axis_index("x"), 3, keepdims=False)
    tok_in = gather_tokens(picked.reshape(2, rows, -1), COL)

    rot = all_sum(dot(tok_out, panel_out, ((2,), (1,))), COL)
    inr = all_sum(dot(tok_in, panel_in, ((2,), (0,))), "x")

    partial_grad = dot(rot[0], inr[0], ((0,), (0,))).astype(bf16)
    grad = total(exchange(partial_grad.reshape(groups, rows_own, -1), DP))
    precond = grad / (eigvals + damping)
    shared = gather(precond.astype(bf16), DP).reshape(groups * rows_own, -1)
    mixed = dot(rot[1], shared, ((1,), (0,)))
    partial_scores = jnp.sum(mixed * inr[1].astype(f32), axis=1)
    scores = lax.psum(lax.psum(partial_scores, COL), "x")
    return precond, scores


def solution(mesh):
    groups, row_count, cols = mesh.devices.shape
    sizes = (4, groups // 4, row_count, 2, cols // 2)
    fine = Mesh(mesh.devices.reshape(sizes), ("y", "z", "x", "h", "c"))
    in_specs = (
        P(("y", "z", "x"), COL),
        P(("y", "z", "h", "c"), None),
        P(COL, ("y", "z", "x")),
        P(("y", "z", "x"), COL),
        P(("y", "z", "x"), COL),
        P(("y", "z", "x"), COL),
        P(("y", "z", "h", "c"), None),
    )
    out_specs = (P(("y", "z", "x"), COL), P(DP))
    return jax.shard_map(
        per_device, mesh=fine, in_specs=in_specs, out_specs=out_specs, check_vma=False
    )
```

```python
import jax
import jax.numpy as jnp
from jax import lax
from jax.sharding import Mesh, PartitionSpec as P

damping = 1.0
f32, bf16 = jnp.float32, jnp.bfloat16
PEERS = ("y", "z1")
COL = ("h", "c")


def exchange(blocks, axes):
    return lax.all_to_all(blocks, axes, 0, 0, tiled=True)


def gather(block, axes):
    count = lax.axis_size(axes)
    return exchange(jnp.broadcast_to(block[None], (count,) + block.shape), axes)


def shift(block, step):
    count = lax.axis_size(("z1", "z0"))
    return lax.ppermute(block, ("z1", "z0"), [(i, (i + step) % count) for i in range(count)])


def swap(block, axis):
    return lax.ppermute(block, axis, [(0, 1), (1, 0)])


def total(blocks):
    return jnp.sum(blocks.astype(f32), axis=0)


def split_tokens(partial, count):
    two, tokens, width = partial.shape
    return partial.reshape(two, count, tokens // count, width).transpose(1, 0, 2, 3)


def join_tokens(parts):
    count, two, rows, width = parts.shape
    return parts.transpose(1, 0, 2, 3).reshape(two, count * rows, width)


def dot(left, right, dims):
    return lax.dot_general(left, right, (dims, ((), ())), preferred_element_type=f32)


def per_device(query_out, query_in, out_basis, in_basis, eigvals, train_out, train_in):
    peers = lax.axis_size(PEERS)
    row_count = lax.axis_size("x")
    rows_own, width = eigvals.shape
    parity, side = lax.axis_index("z0"), lax.axis_index("h")
    flat = (peers * rows_own, width)

    split = jnp.stack([query_in, train_in])
    rows = split.shape[1]
    split = split.reshape(2, rows, peers, 2 * row_count, -1)

    def pick(which):
        index = which * row_count + lax.axis_index("x")
        part = lax.dynamic_index_in_dim(split, index, 3, keepdims=False)
        return part.reshape(2, rows, -1)

    picked = jnp.concatenate([pick(parity), pick(1 - parity)], axis=2)
    far = swap(picked, "h")
    pair = jnp.where(side == 0, jnp.stack([picked, far]), jnp.stack([far, picked]))
    near = gather(pair, "c")
    tok_in = join_tokens(near.transpose(1, 0, 2, 3, 4).reshape((-1,) + near.shape[2:]))
    tok_out = join_tokens(gather(jnp.stack([query_out, train_out]), "x"))

    panel_in = gather(in_basis, PEERS).reshape(flat)
    panel_out = gather(out_basis.T, PEERS).reshape(flat[0], -1)
    panel_in_other = shift(panel_in, 1)
    panel_out_other = shift(panel_out, -1)

    half = flat[0]
    inr = dot(tok_in[..., :half], panel_in, ((2,), (0,)))
    inr = inr + dot(tok_in[..., half:], panel_in_other, ((2,), (0,)))
    inr = total(exchange(split_tokens(inr.astype(bf16), row_count), "x")).astype(bf16)
    inr = join_tokens(gather(inr, "x"))

    panels = jnp.concatenate([panel_out, panel_out_other], axis=0)
    rot = dot(tok_out, panels, ((2,), (1,))).astype(bf16)
    rot = total(exchange(split_tokens(rot, 2), "c")).astype(bf16)
    rot = (rot.astype(f32) + swap(rot, "h").astype(f32)).astype(bf16)
    rot = join_tokens(gather(rot, "c"))

    partial_grad = dot(rot[0], inr[0], ((0,), (0,))).astype(bf16)
    own, other = partial_grad[:half], partial_grad[half:]
    cut = half // 2
    low, high = shift(other[:cut], 1), shift(other[cut:], -1)
    own = own.astype(f32) + jnp.concatenate([low, high], axis=0).astype(f32)
    grad = total(exchange(own.astype(bf16).reshape(peers, rows_own, width), PEERS))
    precond = grad / (eigvals + damping)

    shared = gather(precond.astype(bf16), PEERS).reshape(flat)
    low, high = shift(shared[:cut], 1), shift(shared[cut:], -1)
    mixed = dot(rot[1], jnp.concatenate([shared, low, high], axis=0), ((1,), (0,)))
    partial_scores = jnp.sum(mixed * inr[1].astype(f32), axis=1)
    scores = total(gather(partial_scores, ("x",) + COL))
    return precond, scores


def solution(mesh):
    groups, row_count, cols = mesh.devices.shape
    sizes = (4, groups // 8, 2, row_count, 2, cols // 2)
    fine = Mesh(mesh.devices.reshape(sizes), ("y", "z1", "z0", "x", "h", "c"))
    dp = ("y", "z1", "z0")
    by_rows, by_tokens = P(dp + ("x",), COL), P(dp + COL, None)
    in_specs = (
        by_rows,
        by_tokens,
        P(COL, dp + ("x",)),
        by_rows,
        by_rows,
        by_rows,
        by_tokens,
    )
    return jax.shard_map(
        per_device, mesh=fine, in_specs=in_specs, out_specs=(by_rows, P(dp)), check_vma=False
    )
```

```python
import jax
import jax.numpy as jnp
from jax import lax
from jax.sharding import Mesh, PartitionSpec as P

damping = 1.0
f32, bf16 = jnp.float32, jnp.bfloat16
PEERS = ("y", "z1")
COL = ("h", "c")


def exchange(blocks, axes):
    return lax.all_to_all(blocks, axes, 0, 0, tiled=True)


def gather(block, axes):
    count = lax.axis_size(axes)
    return exchange(jnp.broadcast_to(block[None], (count,) + block.shape), axes)


def shift(block, step):
    count = lax.axis_size(("z1", "z0"))
    return lax.ppermute(block, ("z1", "z0"), [(i, (i + step) % count) for i in range(count)])


def swap(block, axis):
    return lax.ppermute(block, axis, [(0, 1), (1, 0)])


def total(blocks):
    return jnp.sum(blocks.astype(f32), axis=0)


def split_tokens(partial, count):
    two, tokens, width = partial.shape
    return partial.reshape(two, count, tokens // count, width).transpose(1, 0, 2, 3)


def join_tokens(parts):
    count, two, rows, width = parts.shape
    return parts.transpose(1, 0, 2, 3).reshape(two, count * rows, width)


def dot(left, right, dims):
    return lax.dot_general(left, right, (dims, ((), ())), preferred_element_type=f32)


def per_device(query_out, query_in, out_basis, in_basis, eigvals, train_out, train_in):
    peers = lax.axis_size(PEERS)
    row_count = lax.axis_size("x")
    rows_own, width = eigvals.shape
    parity = lax.axis_index("z0")
    flat = (peers * rows_own, width)

    with jax.named_scope("panel_in"):
        panel_in = gather(in_basis, PEERS).reshape(flat)
    with jax.named_scope("near_in"):
        panel_in_other = shift(panel_in, 1)
    basis_rows, panel_in = lax.optimization_barrier((out_basis.T, panel_in))
    with jax.named_scope("panel_out"):
        panel_out = gather(basis_rows, PEERS).reshape(flat[0], -1)
    with jax.named_scope("near_out"):
        panel_out_other = shift(panel_out, -1)

    def pick(tokens):
        split = tokens.T.reshape(peers, 2 * row_count, -1, tokens.shape[0])

        def part(which):
            index = which * row_count + lax.axis_index("x")
            found = lax.dynamic_index_in_dim(split, index, 1, keepdims=False)
            return found.reshape(-1, tokens.shape[0])

        return jnp.concatenate([part(parity), part(1 - parity)], axis=0).T

    def both(block, axis):
        other = swap(block, axis)
        first = lax.axis_index(axis) == 0
        return jnp.where(first, jnp.stack([block, other]), jnp.stack([other, block]))

    with jax.named_scope("pick"):
        picked = jnp.stack([pick(query_in), pick(train_in)])
    with jax.named_scope("tok_in"):
        tok_in = both(both(picked, "c"), "h")
        tok_in = join_tokens(tok_in.reshape((-1,) + picked.shape))
    with jax.named_scope("tok_out"):
        tok_out = join_tokens(gather(jnp.stack([query_out, train_out]), "x"))

    half = flat[0]
    with jax.named_scope("inr"):
        inr = dot(tok_in[..., :half], panel_in, ((2,), (0,)))
        inr = inr + dot(tok_in[..., half:], panel_in_other, ((2,), (0,)))
        inr = total(exchange(split_tokens(inr.astype(bf16), row_count), "x")).astype(bf16)
        inr = join_tokens(gather(inr, "x"))

    with jax.named_scope("rot"):
        panels = jnp.concatenate([panel_out, panel_out_other], axis=0)
        rot = dot(tok_out, panels, ((2,), (1,))).astype(bf16)
        rot = total(exchange(split_tokens(rot, 2), "c")).astype(bf16)
        rot = (rot.astype(f32) + swap(rot, "h").astype(f32)).astype(bf16)
        rot = join_tokens(gather(rot, "c"))

    partial_grad = dot(rot[0], inr[0], ((0,), (0,))).astype(bf16)
    own, other = partial_grad[:half], partial_grad[half:]
    cut = half // 2
    low, high = shift(other[:cut], 1), shift(other[cut:], -1)
    own = own.astype(f32) + jnp.concatenate([low, high], axis=0).astype(f32)
    grad = total(exchange(own.astype(bf16).reshape(peers, rows_own, width), PEERS))
    precond = grad / (eigvals + damping)

    shared = gather(precond.astype(bf16), PEERS).reshape(flat)
    low, high = shift(shared[:cut], 1), shift(shared[cut:], -1)
    mixed = dot(rot[1], jnp.concatenate([shared, low, high], axis=0), ((1,), (0,)))
    partial_scores = jnp.sum(mixed * inr[1].astype(f32), axis=1)
    scores = total(gather(partial_scores, ("x",) + COL))
    return precond, scores


def solution(mesh):
    groups, row_count, cols = mesh.devices.shape
    sizes = (4, groups // 8, 2, row_count, 2, cols // 2)
    fine = Mesh(mesh.devices.reshape(sizes), ("y", "z1", "z0", "x", "h", "c"))
    dp = ("y", "z1", "z0")
    by_rows, by_tokens = P(dp + ("x",), COL), P(dp + COL, None)
    in_specs = (
        by_rows,
        by_tokens,
        P(COL, dp + ("x",)),
        by_rows,
        by_rows,
        by_rows,
        by_tokens,
    )
    return jax.shard_map(
        per_device, mesh=fine, in_specs=in_specs, out_specs=(by_rows, P(dp)), check_vma=False
    )
```

```python
import jax
import jax.numpy as jnp
from jax import lax
from jax.sharding import Mesh, PartitionSpec as P

damping = 1.0
f32, bf16 = jnp.float32, jnp.bfloat16
PEERS = ("y", "z1")
COL = ("h", "c")


def exchange(blocks, axes):
    return lax.all_to_all(blocks, axes, 0, 0, tiled=True)


def gather(block, axes):
    count = lax.axis_size(axes)
    return exchange(jnp.broadcast_to(block[None], (count,) + block.shape), axes)


def shift(block, step):
    count = lax.axis_size(("z1", "z0"))
    return lax.ppermute(block, ("z1", "z0"), [(i, (i + step) % count) for i in range(count)])


def swap(block, axis):
    return lax.ppermute(block, axis, [(0, 1), (1, 0)])


def total(blocks):
    return jnp.sum(blocks.astype(f32), axis=0)


def split_tokens(partial, count):
    two, tokens, width = partial.shape
    return partial.reshape(two, count, tokens // count, width).transpose(1, 0, 2, 3)


def join_tokens(parts):
    count, two, rows, width = parts.shape
    return parts.transpose(1, 0, 2, 3).reshape(two, count * rows, width)


def dot(left, right, dims):
    return lax.dot_general(left, right, (dims, ((), ())), preferred_element_type=f32)


def per_device(query_out, query_in, out_basis, in_basis, eigvals, train_out, train_in):
    peers = lax.axis_size(PEERS)
    row_count = lax.axis_size("x")
    rows_own, width = eigvals.shape
    parity = lax.axis_index("z0")
    half = peers * rows_own

    panels = gather(jnp.concatenate([in_basis, out_basis.T], axis=0), PEERS)

    def pick(tokens):
        split = tokens.T.reshape(peers, 2 * row_count, -1, tokens.shape[0])

        def part(which):
            index = which * row_count + lax.axis_index("x")
            found = lax.dynamic_index_in_dim(split, index, 1, keepdims=False)
            return found.reshape(-1, tokens.shape[0])

        return jnp.concatenate([part(parity), part(1 - parity)], axis=0).T

    def both(block, axis, at):
        other = swap(block, axis)
        first = lax.axis_index(axis) == 0
        return jnp.where(
            first, jnp.stack([block, other], axis=at), jnp.stack([other, block], axis=at)
        )

    picked = jnp.stack([pick(query_in), pick(train_in)])
    pair = both(picked, "h", 0)
    tokens = jnp.stack([query_out, train_out])
    panels, pair, tokens = lax.optimization_barrier((panels, pair, tokens))
    panel_in = panels[:, :rows_own].reshape(half, width)
    panel_out = panels[:, rows_own:].reshape(half, -1)
    panel_in_other = shift(panel_in, 1)
    tok_in = both(pair, "c", 1)
    tok_in = join_tokens(tok_in.reshape((-1,) + picked.shape))
    tok_out = join_tokens(gather(tokens, ("z0", "x")))

    rot = dot(tok_out, panel_out, ((2,), (1,))).astype(bf16)
    rot = total(exchange(split_tokens(rot, 2), "c")).astype(bf16)
    rot = (rot.astype(f32) + swap(rot, "h").astype(f32)).astype(bf16)
    rot = join_tokens(gather(rot, "c"))

    inr = dot(tok_in[..., :half], panel_in, ((2,), (0,)))
    inr = inr + dot(tok_in[..., half:], panel_in_other, ((2,), (0,)))
    inr = total(exchange(split_tokens(inr.astype(bf16), row_count), "x")).astype(bf16)
    inr = join_tokens(gather(inr, ("z0", "x")))

    partial_grad = dot(rot[0], inr[0], ((0,), (0,))).astype(bf16)
    grad = total(exchange(partial_grad.reshape(peers, rows_own, width), PEERS))
    precond = grad / (eigvals + damping)

    shared = gather(precond.astype(bf16), PEERS).reshape(half, width)
    mixed = dot(rot[1], shared, ((1,), (0,)))
    partial_scores = jnp.sum(mixed * inr[1].astype(f32), axis=1)
    adders = ("x",) + COL
    blocks = jnp.broadcast_to(
        partial_scores.reshape(2, 1, -1), (2, lax.axis_size(adders), partial_scores.size // 2)
    )
    blocks = blocks.reshape(-1, 1, partial_scores.size // 2)
    scores = total(exchange(blocks, ("z0",) + adders)).reshape(-1)
    return precond, scores


def solution(mesh):
    groups, row_count, cols = mesh.devices.shape
    sizes = (4, groups // 8, 2, row_count, 2, cols // 2)
    fine = Mesh(mesh.devices.reshape(sizes), ("y", "z1", "z0", "x", "h", "c"))
    dp = ("y", "z1", "z0")
    by_rows, by_tokens = P(dp + ("x",), COL), P(dp + COL, None)
    in_specs = (
        by_rows,
        by_tokens,
        P(COL, dp + ("x",)),
        by_rows,
        by_rows,
        by_rows,
        by_tokens,
    )
    return jax.shard_map(
        per_device, mesh=fine, in_specs=in_specs, out_specs=(by_rows, P(dp)), check_vma=False
    )
```
